32 devices in a mesh: coef: 16 (over z, y, x), rot: 2 (over core).
Axes of the slice: x: 2, y: 2, z: 4, core: 2. Of those that a mesh axis runs over, the one named last changes fastest.
Arguments:
- features: float32 [256, 47872], P(None, 'coef'), may hold values from -200 to 200
- table: float32 [2048, 47872], P('rot', 'coef'), may hold values from -16 to 16
- targets: float32 [256, 2048], P('coef', 'rot'), may hold values from 0 to 1
Outputs:
- grad_features: float32 [256, 47872], P('rot', 'coef')
- grad_table: float32 [2048, 47872], P('rot', 'coef')
The draws below stay inside these ranges and needn't reach their ends.
All inputs are finite; a program needn't handle non-finite values.
Results may differ from the reference program's by a relative error of at most 0.0003.
Values sent between devices are 32-bit elements; how exact they have to be, the bound alone decides.
No kernel may reach another device: no remote copies, remote signals or barrier semaphores. Data moves between devices by JAX's collectives and lax.ppermute only.
A program may use at most 64 MiB of HBM per device.

```python
import jax
import jax.numpy as jnp
from jax import lax

K = 47872
ROTS = 2048
IMGS = 256


def table_parts(key):
    base = jnp.clip(jax.random.normal(jax.random.fold_in(key, 11), (ROTS, K), jnp.float32), -4.0, 4.0)
    shared = jnp.clip(3.0 * jax.random.normal(jax.random.fold_in(key, 13), (1, K), jnp.float32), -7.5, 7.5)
    return base + shared


def draw_table(key, part):
    return table_parts(key)


def draw_features(key, part):
    feats = jnp.clip(jax.random.normal(jax.random.fold_in(key, 21), (IMGS, K), jnp.float32), -5.0, 5.0)
    spread = jax.random.uniform(jax.random.fold_in(key, 22), (IMGS, 1), jnp.float32, jnp.log(0.25), jnp.log(1.0))
    feats = feats * jnp.exp(spread)
    return feats


def draw_targets(key, part):
    labels = jax.random.randint(jax.random.fold_in(key, 31), (IMGS,), 0, ROTS)
    peaks = (labels[:, None] == jnp.arange(ROTS)[None, :]).astype(jnp.float32)
    level = jax.random.uniform(jax.random.fold_in(key, 32), (IMGS, ROTS), jnp.float32, 0.0, 2.0)
    return 0.5 * peaks + 0.5 * level / ROTS


def setup_inputs(seed: int = 0) -> dict:
    key_list = jax.random.split(jax.random.key(seed), 4)
    features = draw_features(jax.random.fold_in(key_list[3], 71), 0)
    table = draw_table(jax.random.fold_in(key_list[3], 71), 0)
    targets = draw_targets(jax.random.fold_in(key_list[3], 71), 0)
    return {"features": features, "table": table, "targets": targets}


logit_gain = 4.0
loss_scale = 64.0

def reference(features, table, targets):
    scale = logit_gain / jnp.sqrt(jnp.float32(K))
    scores = scale * lax.dot_general(features, table, (((1,), (1,)), ((), ())), precision=lax.Precision.HIGHEST, preferred_element_type=jnp.float32)
    row_max = lax.optimization_barrier(jnp.max(scores, axis=1, keepdims=True))
    expo = jnp.exp(scores - row_max)
    probs = expo / lax.optimization_barrier(jnp.sum(expo, axis=1, keepdims=True))
    grad_scores = loss_scale * (probs - targets)
    grad_features = scale * jnp.dot(grad_scores, table, precision=lax.Precision.HIGHEST, preferred_element_type=jnp.float32)
    grad_table = scale * lax.dot_general(grad_scores, features, (((0,), (0,)), ((), ())), precision=lax.Precision.HIGHEST, preferred_element_type=jnp.float32)
    return (grad_features, grad_table)
```

```python
import math

import jax
import jax.numpy as jnp
from jax import lax
from jax.sharding import PartitionSpec as P

logit_gain = 4.0
loss_scale = 64.0


def solution(mesh):
    n = mesh.shape["coef"]
    r = mesh.shape["rot"]
    g = math.gcd(n, 8)
    m = n // g
    inner = [[a * g + b for b in range(g)] for a in range(m)]
    outer = [[a * g + b for a in range(m)] for b in range(g)]
    swap = [(i, (i + g) % n) for i in range(n)]
    rot_swap = [(0, 1), (1, 0)]

    def add_cubes(x):
        if m == 1:
            return x
        if m == 2:
            return x + lax.ppermute(x, "coef", swap)
        return lax.psum(x, "coef", axis_index_groups=outer)

    def join_cubes(x):
        if m == 1:
            return x[None]
        if m == 2:
            other = lax.ppermute(x, "coef", swap)
            first = lax.axis_index("coef") < g
            return jnp.where(first, jnp.stack([x, other]), jnp.stack([other, x]))
        return lax.all_gather(x, "coef", axis_index_groups=outer)

    def on_device(features, table, targets):
        imgs, k = features.shape
        rots = table.shape[0]
        rows = imgs // n
        scale = logit_gain / math.sqrt(k * n)
        high = dict(precision=lax.Precision.HIGH, preferred_element_type=jnp.float32)
        goal = join_cubes(targets)

        partial = lax.dot_general(features, table, (((1,), (1,)), ((), ())), **high)
        blocks = partial.reshape(m, g, rows, rots).transpose(1, 0, 2, 3)
        blocks = lax.all_to_all(blocks, "coef", 0, 0, axis_index_groups=inner, tiled=True)
        scores = scale * add_cubes(jnp.sum(blocks, axis=0))

        top = jnp.max(scores, axis=2, keepdims=True)
        expo = jnp.exp(scores - top)
        total = jnp.sum(expo, axis=2, keepdims=True)
        if r == 2:
            both = jnp.concatenate([top, total], axis=2)
            far = lax.ppermute(both, "rot", rot_swap)
            far_top, far_total = far[:, :, :1], far[:, :, 1:]
            row_max = jnp.maximum(top, far_top)
            ours = jnp.exp(top - row_max)
            row_sum = total * ours + far_total * jnp.exp(far_top - row_max)
        else:
            row_max = lax.pmax(top, "rot")
            ours = jnp.exp(top - row_max)
            row_sum = lax.psum(total * ours, "rot")
        probs = expo * (ours / row_sum)
        grad = (scale * loss_scale) * (probs - goal)

        wide = jnp.broadcast_to(grad[None], (g,) + grad.shape)
        piece = lax.all_to_all(wide, "coef", 0, 0, axis_index_groups=inner, tiled=True)
        piece = piece.transpose(1, 0, 2, 3).reshape(imgs, rots)

        feature_part = jnp.dot(piece, table, **high)
        if r == 2:
            half = imgs // 2
            me = lax.axis_index("rot")
            send = lax.dynamic_slice_in_dim(feature_part, (1 - me) * half, half)
            keep = lax.dynamic_slice_in_dim(feature_part, me * half, half)
            grad_features = keep + lax.ppermute(send, "rot", rot_swap)
        else:
            grad_features = lax.psum_scatter(feature_part, "rot", scatter_dimension=0, tiled=True)
        grad_table = lax.dot_general(piece, features, (((0,), (0,)), ((), ())), **high)
        return (grad_features, grad_table)

    return jax.shard_map(
        on_device,
        mesh=mesh,
        in_specs=(P(None, "coef"), P("rot", "coef"), P("coef", "rot")),
        out_specs=(P("rot", "coef"), P("rot", "coef")),
        check_vma=False,
    )
```

```python
import functools
import math

import jax
import jax.numpy as jnp
from jax import lax
from jax.experimental import pallas as pl
from jax.experimental.pallas import tpu as pltpu
from jax.sharding import PartitionSpec as P

logit_gain = 4.0
loss_scale = 64.0

F32, BF16 = jnp.float32, jnp.bfloat16
HBM = pl.BlockSpec(memory_space=pltpu.HBM)
VMEM = pl.BlockSpec(memory_space=pltpu.VMEM)
CHUNKS = 2


def split(x):
    hi = x.astype(BF16)
    return hi, (x - hi.astype(F32)).astype(BF16)


def product(a, b, da, db):
    return lax.dot_general(a, b, (((da,), (db,)), ((), ())), preferred_element_type=F32)


def cuts_of(k, most):
    return [(a, min(most, k - a)) for a in range(0, k, most)]


def masks_of(g, odd):
    bits = [1 << b for b in range(g.bit_length() - 1)]
    if odd and len(bits) > 1:
        bits[0], bits[1] = bits[1], bits[0]
    return bits


def blocks(g, m):
    me, core = lax.axis_index("coef"), lax.axis_index("rot")
    odd = lax.rem(core, 2)
    inner = lax.rem(me, g)
    found = []
    for q in range(g):
        far = []
        for order in (0, 1):
            steps = masks_of(g, order)
            far.append(sum(bit for s, bit in enumerate(reversed(steps)) if q >> s & 1))
        flip = jnp.where(odd == 1, far[1], far[0])
        for a in range(m):
            found.append(a * g + jnp.bitwise_xor(inner, flip))
    return found


def scores_kernel(g, m, cuts, first, *refs):
    if first:
        feat, table, out, t_hi, t_lo, f_hi, f_lo, feat_v, table_v, acc, sems = refs
    else:
        table, f_hi, f_lo, out, t_hi, t_lo, table_v, acc, sems = refs
    chunk = 0 if first else 1
    width = t_hi.shape[1]
    columns = pl.ds(chunk * width, width)
    copies = []
    for i, (at, size) in enumerate(cuts):
        s = pl.ds(at, size)
        pair = [pltpu.make_async_copy(table.at[s, columns], table_v.at[s], sems.at[0, i])]
        if first:
            pair.append(pltpu.make_async_copy(feat.at[s], feat_v.at[s], sems.at[1, i]))
        for c in pair:
            c.start()
        copies.append(pair)
    for i, (at, size) in enumerate(cuts):
        for c in copies[i]:
            c.wait()
        s = slice(at, at + size)
        if first:
            a_hi, a_lo = split(feat_v[s])
            f_hi[s], f_lo[s] = a_hi, a_lo
        else:
            a_hi, a_lo = f_hi[s], f_lo[s]
        b_hi, b_lo = split(table_v[s])
        t_hi[s], t_lo[s] = b_hi, b_lo
        left = jnp.concatenate([a_hi, a_hi, a_lo], axis=0)
        right = jnp.concatenate([b_hi, b_lo, b_hi], axis=0)
        got = product(left, right, 0, 0)
        if i == 0:
            acc[...] = got
        else:
            acc[...] += got
    rows = acc.shape[0] // (g * m)
    for p, block in enumerate(blocks(g, m)):
        out[p * rows:(p + 1) * rows] = acc[pl.ds(pl.multiple_of(block * rows, rows), rows)]


def scores_call(g, m, table, feat=None, halves=None, depth=512):
    k, rots = table.shape
    first = halves is None
    imgs = (feat if first else halves[0]).shape[1]
    width = rots // CHUNKS
    cuts = cuts_of(k, depth)
    outs = [jax.ShapeDtypeStruct((imgs, width), F32)] + [jax.ShapeDtypeStruct((k, width), BF16)] * 2
    scratch = [pltpu.VMEM((k, width), F32), pltpu.VMEM((imgs, width), F32), pltpu.SemaphoreType.DMA((2, len(cuts)))]
    if first:
        outs += [jax.ShapeDtypeStruct((k, imgs), BF16)] * 2
        scratch = [pltpu.VMEM((k, imgs), F32)] + scratch
    return pl.pallas_call(
        functools.partial(scores_kernel, g, m, cuts, first),
        out_shape=outs,
        in_specs=[HBM, HBM] if first else [HBM, VMEM, VMEM],
        out_specs=[VMEM] * len(outs),
        scratch_shapes=scratch,
        cost_estimate=pl.CostEstimate(flops=6 * k * imgs * width, bytes_accessed=4 * k * width, transcendentals=0),
        compiler_params=pltpu.CompilerParams(vmem_limit_bytes=32 << 20),
        name="scores",
    )(*([feat, table] if first else [table, *halves]))


def table_kernel(g, m, cuts, chunk, *refs):
    f_hi, f_lo, mine, far = refs[:4]
    out, out_v, rhs, sems = refs[-4:]
    imgs, width = rhs.shape[0] // 3, rhs.shape[1]
    n = g * m
    rows = imgs // n
    for p, block in enumerate(blocks(g, m)):
        src, q = (mine, p) if p < n // 2 else (far, p - n // 2)
        hi, lo = split(src[q * rows:(q + 1) * rows])
        for j, part in enumerate((hi, lo, hi)):
            rhs[pl.ds(pl.multiple_of(block * rows + j * imgs, rows), rows)] = part
    copies = []
    for i, (at, size) in enumerate(cuts):
        s = slice(at, at + size)
        a_hi = f_hi[s]
        out_v[s] = product(jnp.concatenate([a_hi, a_hi, f_lo[s]], axis=1), rhs[...], 1, 0)
        copy = pltpu.make_async_copy(
            out_v.at[pl.ds(at, size)],
            out.at[pl.ds(at, size), pl.ds(chunk * width, width)],
            sems.at[i],
        )
        copy.start()
        copies.append(copy)
    for copy in copies:
        copy.wait()


def table_call(g, m, f_hi, f_lo, piece, chunk, onto=None, depth=752):
    k, imgs = f_hi.shape
    width = piece[0].shape[1]
    cuts = cuts_of(k, depth)
    extra = [] if onto is None else [onto]
    return pl.pallas_call(
        functools.partial(table_kernel, g, m, cuts, chunk),
        out_shape=jax.ShapeDtypeStruct((k, width * CHUNKS), F32),
        in_specs=[VMEM] * 4 + [HBM] * len(extra),
        out_specs=HBM,
        scratch_shapes=[
            pltpu.VMEM((k, width), F32),
            pltpu.VMEM((3 * imgs, width), BF16),
            pltpu.SemaphoreType.DMA((len(cuts),)),
        ],
        input_output_aliases={4: 0} if extra else {},
        cost_estimate=pl.CostEstimate(flops=6 * k * imgs * width, bytes_accessed=4 * k * width, transcendentals=0),
        compiler_params=pltpu.CompilerParams(vmem_limit_bytes=24 << 20),
        name="grad_table",
    )(f_hi, f_lo, *piece, *extra)


def features_kernel(g, m, parts, *refs):
    tables, pieces = refs[:2 * CHUNKS], refs[2 * CHUNKS:4 * CHUNKS]
    outs, (rows_v, rhs) = refs[4 * CHUNKS:-2], refs[-2:]
    n = g * m
    imgs, width = rows_v.shape
    rows = imgs // n
    shift = 0 if parts == 1 else (1 - lax.axis_index("rot")) * (n // 2)
    for c in range(CHUNKS):
        mine, far = pieces[2 * c:2 * c + 2]
        for p, block in enumerate(blocks(g, m)):
            src, q = (mine, p) if p < n // 2 else (far, p - n // 2)
            place = lax.rem(block + shift, n)
            rows_v[pl.ds(pl.multiple_of(place * rows, rows), rows)] = src[q * rows:(q + 1) * rows]
        hi, lo = split(rows_v[...].T)
        for j, part in enumerate((hi, lo, hi)):
            rhs[(3 * c + j) * width:(3 * c + j + 1) * width] = part
    left = []
    for c in range(CHUNKS):
        hi, lo = tables[2 * c][...], tables[2 * c + 1][...]
        left += [hi, hi, lo]
    got = product(jnp.concatenate(left, axis=1), rhs[...], 1, 0)
    share = imgs // parts
    for i, out in enumerate(outs):
        out[...] = got[:, i * share:(i + 1) * share]


def features_call(g, m, tables, pieces, parts):
    k, width = tables[0].shape
    imgs = 2 * pieces[0].shape[0]
    return pl.pallas_call(
        functools.partial(features_kernel, g, m, parts),
        out_shape=[jax.ShapeDtypeStruct((k, imgs // parts), F32)] * parts,
        in_specs=[VMEM] * (len(tables) + len(pieces)),
        out_specs=[VMEM] * parts,
        scratch_shapes=[pltpu.VMEM((imgs, width), F32), pltpu.VMEM((3 * CHUNKS * width, imgs), BF16)],
        cost_estimate=pl.CostEstimate(
            flops=6 * k * imgs * width * CHUNKS, bytes_accessed=4 * k * width * CHUNKS, transcendentals=0
        ),
        compiler_params=pltpu.CompilerParams(vmem_limit_bytes=24 << 20),
        name="grad_features",
    )(*tables, *pieces)


def solution(mesh):
    n = mesh.shape["coef"]
    r = mesh.shape["rot"]
    g = math.gcd(n, 8)
    m = n // g
    outer = [[a * g + b for a in range(m)] for b in range(g)]
    swap = [(i, (i + g) % n) for i in range(n)]
    rot_swap = [(0, 1), (1, 0)]
    steps = g.bit_length() - 1

    def exchange(x, step):
        perm = [(i * r + c, (i ^ masks_of(g, c % 2)[step]) * r + c) for i in range(n) for c in range(r)]
        return lax.ppermute(x, ("coef", "rot"), perm)

    def add_cubes(x):
        if m == 1:
            return x
        if m == 2:
            return x + lax.ppermute(x, "coef", swap)
        return lax.psum(x, "coef", axis_index_groups=outer)

    def join_cubes(x):
        if m == 1:
            return x
        if m == 2:
            other = lax.ppermute(x, "coef", swap)
            first = lax.axis_index("coef") < g
            return jnp.where(first, jnp.concatenate([x, other]), jnp.concatenate([other, x]))
        return lax.all_gather(x, "coef", axis_index_groups=outer, tiled=True)

    def reduce(x):
        for step in range(steps):
            half = x.shape[0] // 2
            x = x[:half] + exchange(x[half:], step)
        return add_cubes(x)

    def gather(x):
        for step in reversed(range(1, steps)):
            x = jnp.concatenate([x, exchange(x, step)])
        return x, exchange(x, 0)

    def on_device(features, table, targets):
        imgs, k = features.shape
        rots = table.shape[0]
        width = rots // CHUNKS
        scale = logit_gain / math.sqrt(k * n)
        features, table = features.T, table.T
        goal = join_cubes(targets)

        first, *rest = scores_call(g, m, table, feat=features)
        tables, halves = rest[:2], rest[2:]
        second, *more = scores_call(g, m, table, halves=halves)
        tables = tables + more
        scores = [scale * reduce(part) for part in (first, second)]

        top = functools.reduce(jnp.maximum, [jnp.max(s, axis=1, keepdims=True) for s in scores])
        expo = [jnp.exp(s - top) for s in scores]
        total = sum(jnp.sum(e, axis=1, keepdims=True) for e in expo)
        if r == 2:
            both = jnp.concatenate([top, total], axis=1)
            far = lax.ppermute(both, "rot", rot_swap)
            far_top, far_total = far[:, :1], far[:, 1:]
            row_max = jnp.maximum(top, far_top)
            ours = jnp.exp(top - row_max)
            row_sum = total * ours + far_total * jnp.exp(far_top - row_max)
        else:
            row_max = lax.pmax(top, "rot")
            ours = jnp.exp(top - row_max)
            row_sum = lax.psum(total * ours, "rot")
        norm = ours / row_sum
        pieces = []
        for c, e in enumerate(expo):
            grad = (scale * loss_scale) * (e * norm - goal[:, c * width:(c + 1) * width])
            pieces.append(gather(grad))

        grad_table = table_call(g, m, *halves, pieces[0], 0)
        flat = [x for piece in pieces for x in piece]
        if r == 2:
            send, keep = features_call(g, m, tables, flat, 2)
            grad_features = keep + lax.ppermute(send, "rot", rot_swap)
        else:
            (whole,) = features_call(g, m, tables, flat, 1)
            grad_features = lax.psum_scatter(whole, "rot", scatter_dimension=1, tiled=True)
        grad_table = table_call(g, m, *halves, pieces[1], 1, grad_table)
        return (grad_features.T, grad_table.T)

    return jax.shard_map(
        on_device,
        mesh=mesh,
        in_specs=(P(None, "coef"), P("rot", "coef"), P("coef", "rot")),
        out_specs=(P("rot", "coef"), P("rot", "coef")),
        check_vma=False,
    )
```

```python
import functools
import math

import jax
import jax.numpy as jnp
from jax import lax
from jax.experimental import pallas as pl
from jax.experimental.pallas import tpu as pltpu
from jax.sharding import PartitionSpec as P

logit_gain = 4.0
loss_scale = 64.0

F32, BF16 = jnp.float32, jnp.bfloat16
HBM = pl.BlockSpec(memory_space=pltpu.HBM)
VMEM = pl.BlockSpec(memory_space=pltpu.VMEM)
CHUNKS = 2


def split(x):
    hi = x.astype(BF16)
    return hi, (x - hi.astype(F32)).astype(BF16)


def product(a, b, da, db):
    return lax.dot_general(a, b, (((da,), (db,)), ((), ())), preferred_element_type=F32)


def cuts_of(k, most):
    return [(a, min(most, k - a)) for a in range(0, k, most)]


def masks_of(g, odd):
    bits = [1 << b for b in range(g.bit_length() - 1)]
    if odd and len(bits) > 1:
        bits[0], bits[1] = bits[1], bits[0]
    return bits


def blocks(g, m):
    me, core = lax.axis_index("coef"), lax.axis_index("rot")
    odd = lax.rem(core, 2)
    inner = lax.rem(me, g)
    found = []
    for q in range(g):
        far = []
        for order in (0, 1):
            steps = masks_of(g, order)
            far.append(sum(bit for s, bit in enumerate(reversed(steps)) if q >> s & 1))
        flip = jnp.where(odd == 1, far[1], far[0])
        for a in range(m):
            found.append(a * g + jnp.bitwise_xor(inner, flip))
    return found


def scores_kernel(g, m, cuts, first, *refs):
    if first:
        feat, table, keep, send, f_hi, f_lo, feat_v, table_v, acc, sems = refs
    else:
        table, f_hi, f_lo, keep, send, table_v, acc, sems = refs
    chunk = 0 if first else 1
    width = keep.shape[1]
    columns = pl.ds(chunk * width, width)
    copies = []
    for i, (at, size) in enumerate(cuts):
        s = pl.ds(at, size)
        pair = [pltpu.make_async_copy(table.at[s, columns], table_v.at[s], sems.at[0, i])]
        if first:
            pair.append(pltpu.make_async_copy(feat.at[s], feat_v.at[s], sems.at[1, i]))
        for c in pair:
            c.start()
        copies.append(pair)
    for i, (at, size) in enumerate(cuts):
        for c in copies[i]:
            c.wait()
        s = slice(at, at + size)
        if first:
            a_hi, a_lo = split(feat_v[s])
            f_hi[s], f_lo[s] = a_hi, a_lo
        else:
            a_hi, a_lo = f_hi[s], f_lo[s]
        b_hi, b_lo = split(table_v[s])
        left = jnp.concatenate([a_hi, a_hi, a_lo], axis=0)
        right = jnp.concatenate([b_hi, b_lo, b_hi], axis=0)
        got = product(left, right, 0, 0)
        if i == 0:
            acc[...] = got
        else:
            acc[...] += got
    rows = acc.shape[0] // (g * m)
    half = g * m // 2
    for p, block in enumerate(blocks(g, m)):
        out, q = (keep, p) if p < half else (send, p - half)
        out[q * rows:(q + 1) * rows] = acc[pl.ds(pl.multiple_of(block * rows, rows), rows)]


def scores_call(g, m, table, feat=None, halves=None, depth=512):
    k, rots = table.shape
    first = halves is None
    imgs = (feat if first else halves[0]).shape[1]
    width = rots // CHUNKS
    cuts = cuts_of(k, depth)
    outs = [jax.ShapeDtypeStruct((imgs // 2, width), F32)] * 2
    scratch = [pltpu.VMEM((k, width), F32), pltpu.VMEM((imgs, width), F32), pltpu.SemaphoreType.DMA((2, len(cuts)))]
    if first:
        outs += [jax.ShapeDtypeStruct((k, imgs), BF16)] * 2
        scratch = [pltpu.VMEM((k, imgs), F32)] + scratch
    return pl.pallas_call(
        functools.partial(scores_kernel, g, m, cuts, first),
        out_shape=outs,
        in_specs=[HBM, HBM] if first else [HBM, VMEM, VMEM],
        out_specs=[VMEM] * len(outs),
        scratch_shapes=scratch,
        cost_estimate=pl.CostEstimate(flops=6 * k * imgs * width, bytes_accessed=4 * k * width, transcendentals=0),
        compiler_params=pltpu.CompilerParams(vmem_limit_bytes=32 << 20),
        name="scores",
    )(*([feat, table] if first else [table, *halves]))


def load_all(src, dst, cuts, sems):
    copies = [pltpu.make_async_copy(src.at[pl.ds(*cut)], dst.at[pl.ds(*cut)], sems.at[i]) for i, cut in enumerate(cuts)]
    for copy in copies:
        copy.start()
    return copies


def table_kernel(g, m, cuts, chunk, *refs):
    feat, mine, far = refs[:3]
    out, feat_v, out_v, rhs, in_sems, out_sems = refs[-6:]
    loads = load_all(feat, feat_v, cuts, in_sems)
    imgs, width = rhs.shape[0] // 3, rhs.shape[1]
    n = g * m
    rows = imgs // n
    for p, block in enumerate(blocks(g, m)):
        src, q = (mine, p) if p < n // 2 else (far, p - n // 2)
        hi, lo = split(src[q * rows:(q + 1) * rows])
        for j, part in enumerate((hi, lo, hi)):
            rhs[pl.ds(pl.multiple_of(block * rows + j * imgs, rows), rows)] = part
    copies = []
    for i, (at, size) in enumerate(cuts):
        loads[i].wait()
        s = slice(at, at + size)
        hi, lo = split(feat_v[s])
        out_v[s] = product(jnp.concatenate([hi, hi, lo], axis=1), rhs[...], 1, 0)
        copy = pltpu.make_async_copy(
            out_v.at[pl.ds(at, size)],
            out.at[pl.ds(at, size), pl.ds(chunk * width, width)],
            out_sems.at[i],
        )
        copy.start()
        copies.append(copy)
    for copy in copies:
        copy.wait()


def table_call(g, m, feat, piece, chunk, onto=None, depth=752):
    k, imgs = feat.shape
    width = piece[0].shape[1]
    cuts = cuts_of(k, depth)
    extra = [] if onto is None else [onto]
    return pl.pallas_call(
        functools.partial(table_kernel, g, m, cuts, chunk),
        out_shape=jax.ShapeDtypeStruct((k, width * CHUNKS), F32),
        in_specs=[HBM, VMEM, VMEM] + [HBM] * len(extra),
        out_specs=HBM,
        scratch_shapes=[
            pltpu.VMEM((k, imgs), F32),
            pltpu.VMEM((k, width), F32),
            pltpu.VMEM((3 * imgs, width), BF16),
            pltpu.SemaphoreType.DMA((len(cuts),)),
            pltpu.SemaphoreType.DMA((len(cuts),)),
        ],
        input_output_aliases={3: 0} if extra else {},
        cost_estimate=pl.CostEstimate(flops=6 * k * imgs * width, bytes_accessed=4 * k * width, transcendentals=0),
        compiler_params=pltpu.CompilerParams(vmem_limit_bytes=24 << 20),
        name="grad_table",
    )(feat, *piece, *extra)


def features_kernel(g, m, cuts, parts, *refs):
    table, pieces = refs[0], refs[1:1 + 2 * CHUNKS]
    outs, (table_v, rows_v, rhs, sems) = refs[2 + 2 * CHUNKS:-4], refs[-4:]
    loads = load_all(table, table_v, cuts, sems)
    n = g * m
    imgs, width = rows_v.shape
    rows = imgs // n
    rots = width * CHUNKS
    shift = 0 if parts == 1 else (1 - lax.axis_index("rot")) * (n // 2)
    for c in range(CHUNKS):
        mine, far = pieces[2 * c:2 * c + 2]
        for p, block in enumerate(blocks(g, m)):
            src, q = (mine, p) if p < n // 2 else (far, p - n // 2)
            place = lax.rem(block + shift, n)
            rows_v[pl.ds(pl.multiple_of(place * rows, rows), rows)] = src[q * rows:(q + 1) * rows]
        hi, lo = split(rows_v[...].T)
        for j, part in enumerate((hi, lo, hi)):
            rhs[j * rots + c * width:j * rots + (c + 1) * width] = part
    share = imgs // parts
    for i, (at, size) in enumerate(cuts):
        loads[i].wait()
        s = slice(at, at + size)
        hi, lo = split(table_v[s])
        got = product(jnp.concatenate([hi, hi, lo], axis=1), rhs[...], 1, 0)
        for j, out in enumerate(outs):
            out[s] = got[:, j * share:(j + 1) * share]


def features_call(g, m, table, pieces, parts, after, head=256, depth=912):
    k, rots = table.shape
    imgs = 2 * pieces[0].shape[0]
    head = min(head, k)
    cuts = [(0, head)] + [(head + at, size) for at, size in cuts_of(k - head, depth)]
    return pl.pallas_call(
        functools.partial(features_kernel, g, m, cuts, parts),
        out_shape=[jax.ShapeDtypeStruct((k, imgs // parts), F32)] * parts,
        in_specs=[HBM] + [VMEM] * len(pieces) + [HBM],
        out_specs=[VMEM] * parts,
        scratch_shapes=[
            pltpu.VMEM((k, rots), F32),
            pltpu.VMEM((imgs, rots // CHUNKS), F32),
            pltpu.VMEM((3 * rots, imgs), BF16),
            pltpu.SemaphoreType.DMA((len(cuts),)),
        ],
        cost_estimate=pl.CostEstimate(flops=6 * k * imgs * rots, bytes_accessed=4 * k * rots, transcendentals=0),
        compiler_params=pltpu.CompilerParams(vmem_limit_bytes=40 << 20),
        name="grad_features",
    )(table, *pieces, after)


def solution(mesh):
    n = mesh.shape["coef"]
    r = mesh.shape["rot"]
    g = math.gcd(n, 8)
    m = n // g
    outer = [[a * g + b for a in range(m)] for b in range(g)]
    swap = [(i, (i + g) % n) for i in range(n)]
    rot_swap = [(0, 1), (1, 0)]
    steps = g.bit_length() - 1

    def exchange(x, step):
        perm = [(i * r + c, (i ^ masks_of(g, c % 2)[step]) * r + c) for i in range(n) for c in range(r)]
        return lax.ppermute(x, ("coef", "rot"), perm)

    def add_cubes(x):
        if m == 1:
            return x
        if m == 2:
            return x + lax.ppermute(x, "coef", swap)
        return lax.psum(x, "coef", axis_index_groups=outer)

    def join_cubes(x):
        if m == 1:
            return x
        if m == 2:
            other = lax.ppermute(x, "coef", swap)
            first = lax.axis_index("coef") < g
            return jnp.where(first, jnp.concatenate([x, other]), jnp.concatenate([other, x]))
        return lax.all_gather(x, "coef", axis_index_groups=outer, tiled=True)

    def reduce(keep, send):
        x = keep + exchange(send, 0)
        for step in range(1, steps):
            half = x.shape[0] // 2
            x = x[:half] + exchange(x[half:], step)
        return add_cubes(x)

    def gather(x):
        for step in reversed(range(1, steps)):
            x = jnp.concatenate([x, exchange(x, step)])
        return x, exchange(x, 0)

    def on_device(features, table, targets):
        imgs, k = features.shape
        rots = table.shape[0]
        width = rots // CHUNKS
        scale = logit_gain / math.sqrt(k * n)
        features = pltpu.with_memory_space_constraint(features.T, pltpu.HBM)
        table = pltpu.with_memory_space_constraint(table.T, pltpu.HBM)
        goal = join_cubes(targets)

        keep, send, *halves = scores_call(g, m, table, feat=features)
        scores = [scale * reduce(keep, send), scale * reduce(*scores_call(g, m, table, halves=halves))]

        top = functools.reduce(jnp.maximum, [jnp.max(s, axis=1, keepdims=True) for s in scores])
        expo = [jnp.exp(s - top) for s in scores]
        total = sum(jnp.sum(e, axis=1, keepdims=True) for e in expo)
        if r == 2:
            both = jnp.concatenate([top, total], axis=1)
            far = lax.ppermute(both, "rot", rot_swap)
            far_top, far_total = far[:, :1], far[:, 1:]
            row_max = jnp.maximum(top, far_top)
            ours = jnp.exp(top - row_max)
            row_sum = total * ours + far_total * jnp.exp(far_top - row_max)
        else:
            row_max = lax.pmax(top, "rot")
            ours = jnp.exp(top - row_max)
            row_sum = lax.psum(total * ours, "rot")
        norm = ours / row_sum
        pieces = []
        for c, e in enumerate(expo):
            grad = (scale * loss_scale) * (e * norm - goal[:, c * width:(c + 1) * width])
            pieces.append(gather(grad))

        grad_table = table_call(g, m, features, pieces[0], 0)
        flat = [x for piece in pieces for x in piece]
        if r == 2:
            send, keep = features_call(g, m, table, flat, 2, grad_table)
            grad_features = keep + lax.ppermute(send, "rot", rot_swap)
        else:
            (whole,) = features_call(g, m, table, flat, 1, grad_table)
            grad_features = lax.psum_scatter(whole, "rot", scatter_dimension=1, tiled=True)
        grad_table = table_call(g, m, features, pieces[1], 1, grad_table)
        return (grad_features.T, grad_table.T)

    return jax.shard_map(
        on_device,
        mesh=mesh,
        in_specs=(P(None, "coef"), P("rot", "coef"), P("coef", "rot")),
        out_specs=(P("rot", "coef"), P("rot", "coef")),
        check_vma=False,
    )
```

```python
import functools
import math

import jax
import jax.numpy as jnp
from jax import lax
from jax.experimental import pallas as pl
from jax.experimental.pallas import tpu as pltpu
from jax.sharding import PartitionSpec as P

logit_gain = 4.0
loss_scale = 64.0

F32, BF16 = jnp.float32, jnp.bfloat16
HBM = pl.BlockSpec(memory_space=pltpu.HBM)
VMEM = pl.BlockSpec(memory_space=pltpu.VMEM)
CHUNKS = 2


def split(x):
    hi = x.astype(BF16)
    return hi, (x - hi.astype(F32)).astype(BF16)


def product(a, b, da, db):
    return lax.dot_general(a, b, (((da,), (db,)), ((), ())), preferred_element_type=F32)


def cuts_of(k, most):
    return [(a, min(most, k - a)) for a in range(0, k, most)]


def masks_of(g, odd):
    bits = [1 << b for b in range(g.bit_length() - 1)]
    if odd and len(bits) > 1:
        bits[0], bits[1] = bits[1], bits[0]
    return bits


def blocks(g, m):
    me, core = lax.axis_index("coef"), lax.axis_index("rot")
    odd = lax.rem(core, 2)
    inner = lax.rem(me, g)
    found = []
    for q in range(g):
        far = []
        for order in (0, 1):
            steps = masks_of(g, order)
            far.append(sum(bit for s, bit in enumerate(reversed(steps)) if q >> s & 1))
        flip = jnp.where(odd == 1, far[1], far[0])
        for a in range(m):
            found.append(a * g + jnp.bitwise_xor(inner, flip))
    return found


def scores_kernel(g, m, cuts, first, *refs):
    if first:
        feat, table, keep, send, t_hi, t_lo, f_hi, f_lo, feat_v, table_v, acc, sems = refs
    else:
        table, f_hi, f_lo, keep, send, t_hi, t_lo, table_v, acc, sems = refs
    chunk = 0 if first else 1
    width = keep.shape[1]
    columns = pl.ds(chunk * width, width)
    copies = []
    for i, (at, size) in enumerate(cuts):
        s = pl.ds(at, size)
        pair = [pltpu.make_async_copy(table.at[s, columns], table_v.at[s], sems.at[0, i])]
        if first:
            pair.append(pltpu.make_async_copy(feat.at[s], feat_v.at[s], sems.at[1, i]))
        for c in pair:
            c.start()
        copies.append(pair)
    for i, (at, size) in enumerate(cuts):
        for c in copies[i]:
            c.wait()
        s = slice(at, at + size)
        if first:
            a_hi, a_lo = split(feat_v[s])
            f_hi[s], f_lo[s] = a_hi, a_lo
        else:
            a_hi, a_lo = f_hi[s], f_lo[s]
        b_hi, b_lo = split(table_v[s])
        t_hi[s], t_lo[s] = b_hi, b_lo
        left = jnp.concatenate([a_hi, a_hi, a_lo], axis=0)
        right = jnp.concatenate([b_hi, b_lo, b_hi], axis=0)
        got = product(left, right, 0, 0)
        if i == 0:
            acc[...] = got
        else:
            acc[...] += got
    rows = acc.shape[0] // (g * m)
    half = g * m // 2
    for p, block in enumerate(blocks(g, m)):
        out, q = (keep, p) if p < half else (send, p - half)
        out[q * rows:(q + 1) * rows] = acc[pl.ds(pl.multiple_of(block * rows, rows), rows)]


def scores_call(g, m, table, feat=None, halves=None, depth=512):
    k, rots = table.shape
    first = halves is None
    imgs = (feat if first else halves[0]).shape[1]
    width = rots // CHUNKS
    cuts = cuts_of(k, depth)
    outs = [jax.ShapeDtypeStruct((imgs // 2, width), F32)] * 2 + [jax.ShapeDtypeStruct((k, width), BF16)] * 2
    scratch = [pltpu.VMEM((k, width), F32), pltpu.VMEM((imgs, width), F32), pltpu.SemaphoreType.DMA((2, len(cuts)))]
    if first:
        outs += [jax.ShapeDtypeStruct((k, imgs), BF16)] * 2
        scratch = [pltpu.VMEM((k, imgs), F32)] + scratch
    return pl.pallas_call(
        functools.partial(scores_kernel, g, m, cuts, first),
        out_shape=outs,
        in_specs=[HBM, HBM] if first else [HBM, VMEM, VMEM],
        out_specs=[VMEM] * len(outs),
        scratch_shapes=scratch,
        cost_estimate=pl.CostEstimate(flops=6 * k * imgs * width, bytes_accessed=4 * k * width, transcendentals=0),
        compiler_params=pltpu.CompilerParams(vmem_limit_bytes=20 << 20),
        name="scores",
    )(*([feat, table] if first else [table, *halves]))


def table_kernel(g, m, cuts, chunk, *refs):
    f_hi, f_lo, mine, far = refs[:4]
    out, token, out_v, rhs, sems = refs[-5:]
    token[...] = jnp.zeros_like(token)
    imgs, width = rhs.shape[0] // 3, rhs.shape[1]
    n = g * m
    rows = imgs // n
    for p, block in enumerate(blocks(g, m)):
        src, q = (mine, p) if p < n // 2 else (far, p - n // 2)
        hi, lo = split(src[q * rows:(q + 1) * rows])
        for j, part in enumerate((hi, lo, hi)):
            rhs[pl.ds(pl.multiple_of(block * rows + j * imgs, rows), rows)] = part
    copies = []
    for i, (at, size) in enumerate(cuts):
        s = slice(at, at + size)
        a_hi = f_hi[s]
        out_v[s] = product(jnp.concatenate([a_hi, a_hi, f_lo[s]], axis=1), rhs[...], 1, 0)
        copy = pltpu.make_async_copy(
            out_v.at[pl.ds(at, size)],
            out.at[pl.ds(at, size), pl.ds(chunk * width, width)],
            sems.at[i],
        )
        copy.start()
        copies.append(copy)
    for copy in copies:
        copy.wait()


def table_call(g, m, f_hi, f_lo, piece, chunk, onto=None, depth=752):
    k, imgs = f_hi.shape
    width = piece[0].shape[1]
    cuts = cuts_of(k, depth)
    extra = [] if onto is None else [onto]
    return pl.pallas_call(
        functools.partial(table_kernel, g, m, cuts, chunk),
        out_shape=[jax.ShapeDtypeStruct((k, width * CHUNKS), F32), jax.ShapeDtypeStruct((8, 128), F32)],
        in_specs=[VMEM] * 4 + [HBM] * len(extra),
        out_specs=[HBM, VMEM],
        scratch_shapes=[
            pltpu.VMEM((k, width), F32),
            pltpu.VMEM((3 * imgs, width), BF16),
            pltpu.SemaphoreType.DMA((len(cuts),)),
        ],
        input_output_aliases={4: 0} if extra else {},
        cost_estimate=pl.CostEstimate(flops=6 * k * imgs * width, bytes_accessed=4 * k * width, transcendentals=0),
        compiler_params=pltpu.CompilerParams(vmem_limit_bytes=24 << 20),
        name="grad_table",
    )(f_hi, f_lo, *piece, *extra)


def features_kernel(g, m, parts, *refs):
    tables, pieces = refs[:2 * CHUNKS], refs[2 * CHUNKS:4 * CHUNKS]
    outs, (rows_v, rhs) = refs[4 * CHUNKS + 1:-2], refs[-2:]
    n = g * m
    imgs, width = rows_v.shape
    rows = imgs // n
    shift = 0 if parts == 1 else (1 - lax.axis_index("rot")) * (n // 2)
    for c in range(CHUNKS):
        mine, far = pieces[2 * c:2 * c + 2]
        for p, block in enumerate(blocks(g, m)):
            src, q = (mine, p) if p < n // 2 else (far, p - n // 2)
            place = lax.rem(block + shift, n)
            rows_v[pl.ds(pl.multiple_of(place * rows, rows), rows)] = src[q * rows:(q + 1) * rows]
        hi, lo = split(rows_v[...].T)
        for j, part in enumerate((hi, lo, hi)):
            rhs[(3 * c + j) * width:(3 * c + j + 1) * width] = part
    left = []
    for c in range(CHUNKS):
        hi, lo = tables[2 * c][...], tables[2 * c + 1][...]
        left += [hi, hi, lo]
    got = product(jnp.concatenate(left, axis=1), rhs[...], 1, 0)
    share = imgs // parts
    for i, out in enumerate(outs):
        out[...] = got[:, i * share:(i + 1) * share]


def features_call(g, m, tables, pieces, parts, after):
    k, width = tables[0].shape
    imgs = 2 * pieces[0].shape[0]
    return pl.pallas_call(
        functools.partial(features_kernel, g, m, parts),
        out_shape=[jax.ShapeDtypeStruct((k, imgs // parts), F32)] * parts,
        in_specs=[VMEM] * (len(tables) + len(pieces) + 1),
        out_specs=[VMEM] * parts,
        scratch_shapes=[pltpu.VMEM((imgs, width), F32), pltpu.VMEM((3 * CHUNKS * width, imgs), BF16)],
        cost_estimate=pl.CostEstimate(
            flops=6 * k * imgs * width * CHUNKS, bytes_accessed=4 * k * width * CHUNKS, transcendentals=0
        ),
        compiler_params=pltpu.CompilerParams(vmem_limit_bytes=24 << 20),
        name="grad_features",
    )(*tables, *pieces, after)


def join_kernel(g, mine, other, out):
    rows = mine.shape[0]
    cube = lax.div(lax.axis_index("coef"), g)
    out[pl.ds(pl.multiple_of(cube * rows, rows), rows)] = mine[...]
    out[pl.ds(pl.multiple_of((1 - cube) * rows, rows), rows)] = other[...]


def join_call(g, mine, other):
    rows, cols = mine.shape
    return pl.pallas_call(
        functools.partial(join_kernel, g),
        out_shape=jax.ShapeDtypeStruct((2 * rows, cols), mine.dtype),
        in_specs=[VMEM] * 2,
        out_specs=VMEM,
        compiler_params=pltpu.CompilerParams(vmem_limit_bytes=4 << 20),
        name="join",
    )(mine, other)


def solution(mesh):
    n = mesh.shape["coef"]
    r = mesh.shape["rot"]
    g = math.gcd(n, 8)
    m = n // g
    outer = [[a * g + b for a in range(m)] for b in range(g)]
    swap = [(i, (i + g) % n) for i in range(n)]
    rot_swap = [(0, 1), (1, 0)]
    steps = g.bit_length() - 1

    def exchange(x, step):
        perm = [(i * r + c, (i ^ masks_of(g, c % 2)[step]) * r + c) for i in range(n) for c in range(r)]
        return lax.ppermute(x, ("coef", "rot"), perm)

    def add_cubes(x):
        if m == 1:
            return x
        if m == 2:
            return x + lax.ppermute(x, "coef", swap)
        return lax.psum(x, "coef", axis_index_groups=outer)

    def join_cubes(x):
        if m == 1:
            return x
        if m == 2:
            return join_call(g, x, lax.ppermute(x, "coef", swap))
        return lax.all_gather(x, "coef", axis_index_groups=outer, tiled=True)

    def reduce(keep, send):
        x = keep + exchange(send, 0)
        for step in range(1, steps):
            half = x.shape[0] // 2
            x = x[:half] + exchange(x[half:], step)
        return add_cubes(x)

    def gather(x):
        for step in reversed(range(1, steps)):
            x = jnp.concatenate([x, exchange(x, step)])
        return x, exchange(x, 0)

    def on_device(features, table, targets):
        imgs, k = features.shape
        rots = table.shape[0]
        width = rots // CHUNKS
        scale = logit_gain / math.sqrt(k * n)
        features = pltpu.with_memory_space_constraint(features.T, pltpu.HBM)
        table = pltpu.with_memory_space_constraint(table.T, pltpu.HBM)
        goal = join_cubes(targets)

        keep, send, *rest = scores_call(g, m, table, feat=features)
        tables, halves = rest[:2], rest[2:]
        last_keep, last_send, *more = scores_call(g, m, table, halves=halves)
        tables = tables + more
        scores = [scale * reduce(keep, send), scale * reduce(last_keep, last_send)]

        top = functools.reduce(jnp.maximum, [jnp.max(s, axis=1, keepdims=True) for s in scores])
        expo = [jnp.exp(s - top) for s in scores]
        total = sum(jnp.sum(e, axis=1, keepdims=True) for e in expo)
        if r == 2:
            both = jnp.concatenate([top, total], axis=1)
            far = lax.ppermute(both, "rot", rot_swap)
            far_top, far_total = far[:, :1], far[:, 1:]
            row_max = jnp.maximum(top, far_top)
            ours = jnp.exp(top - row_max)
            row_sum = total * ours + far_total * jnp.exp(far_top - row_max)
        else:
            row_max = lax.pmax(top, "rot")
            ours = jnp.exp(top - row_max)
            row_sum = lax.psum(total * ours, "rot")
        norm = ours / row_sum
        pieces = []
        for c, e in enumerate(expo):
            grad = (scale * loss_scale) * (e * norm - goal[:, c * width:(c + 1) * width])
            pieces.append(gather(grad))

        grad_table, done = table_call(g, m, *halves, pieces[0], 0)
        flat = [x for piece in pieces for x in piece]
        if r == 2:
            send, keep = features_call(g, m, tables, flat, 2, done)
            grad_features = keep + lax.ppermute(send, "rot", rot_swap)
        else:
            (whole,) = features_call(g, m, tables, flat, 1, done)
            grad_features = lax.psum_scatter(whole, "rot", scatter_dimension=1, tiled=True)
        grad_table, _ = table_call(g, m, *halves, pieces[1], 1, grad_table)
        return (grad_features.T, grad_table.T)

    return jax.shard_map(
        on_device,
        mesh=mesh,
        in_specs=(P(None, "coef"), P("rot", "coef"), P("coef", "rot")),
        out_specs=(P("rot", "coef"), P("rot", "coef")),
        check_vma=False,
    )
```

```python
import functools
import math

import jax
import jax.numpy as jnp
from jax import lax
from jax.experimental import pallas as pl
from jax.experimental.pallas import tpu as pltpu
from jax.sharding import PartitionSpec as P

logit_gain = 4.0
loss_scale = 64.0

F32, BF16 = jnp.float32, jnp.bfloat16
HBM = pl.BlockSpec(memory_space=pltpu.HBM)
VMEM = pl.BlockSpec(memory_space=pltpu.VMEM)
CHUNKS = 2


def split(x):
    hi = x.astype(BF16)
    return hi, (x - hi.astype(F32)).astype(BF16)


def product(a, b, da, db):
    return lax.dot_general(a, b, (((da,), (db,)), ((), ())), preferred_element_type=F32)


def cuts_of(k, most):
    return [(a, min(most, k - a)) for a in range(0, k, most)]


ORDERS = {
    "scores0": ((0, 2, 1), (1, 2, 0)),
    "scores1": ((0, 1, 2), (1, 2, 0)),
    "grads0": ((0, 1, 2), (1, 2, 0)),
    "grads1": ((0, 1, 2), (1, 2, 0)),
}


def masks_of(g, use, odd):
    return [1 << b for b in ORDERS[use][odd] if 1 << b < g]


def blocks(g, m, use):
    me, core = lax.axis_index("coef"), lax.axis_index("rot")
    odd = lax.rem(core, 2)
    inner = lax.rem(me, g)
    found = []
    for q in range(g):
        far = []
        for order in (0, 1):
            steps = masks_of(g, use, order)
            far.append(sum(bit for s, bit in enumerate(reversed(steps)) if q >> s & 1))
        flip = jnp.where(odd == 1, far[1], far[0])
        for a in range(m):
            found.append(a * g + jnp.bitwise_xor(inner, flip))
    return found


def scores_kernel(g, m, cuts, first, *refs):
    if first:
        feat, table, keep, send, t_hi, t_lo, f_hi, f_lo, feat_v, table_v, acc, sems = refs
    else:
        table_v, f_hi, f_lo, keep, send, t_hi, t_lo, acc = refs
    width = keep.shape[1]
    copies = [[] for _ in cuts]
    if first:
        for i, (at, size) in enumerate(cuts):
            s = pl.ds(at, size)
            copies[i] = [
                pltpu.make_async_copy(table.at[s, pl.ds(0, width)], table_v.at[s], sems.at[0, i]),
                pltpu.make_async_copy(feat.at[s], feat_v.at[s], sems.at[1, i]),
            ]
            for c in copies[i]:
                c.start()
    for i, (at, size) in enumerate(cuts):
        for c in copies[i]:
            c.wait()
        s = slice(at, at + size)
        if first:
            a_hi, a_lo = split(feat_v[s])
            f_hi[s], f_lo[s] = a_hi, a_lo
        else:
            a_hi, a_lo = f_hi[s], f_lo[s]
        b_hi, b_lo = split(table_v[s] if first else table_v[s, width:2 * width])
        t_hi[s], t_lo[s] = b_hi, b_lo
        left = jnp.concatenate([a_hi, a_hi, a_lo], axis=0)
        right = jnp.concatenate([b_hi, b_lo, b_hi], axis=0)
        got = product(left, right, 0, 0)
        if i == 0:
            acc[...] = got
        else:
            acc[...] += got
    rows = acc.shape[0] // (g * m)
    half = g * m // 2
    for p, block in enumerate(blocks(g, m, "scores0" if first else "scores1")):
        out, q = (keep, p) if p < half else (send, p - half)
        out[q * rows:(q + 1) * rows] = acc[pl.ds(pl.multiple_of(block * rows, rows), rows)]


def scores_call(g, m, table, feat=None, halves=None, depth=512):
    first = halves is None
    k, width = table.shape
    width //= CHUNKS
    imgs = (feat if first else halves[0]).shape[1]
    cuts = cuts_of(k, depth)
    outs = [jax.ShapeDtypeStruct((imgs // 2, width), F32)] * 2 + [jax.ShapeDtypeStruct((k, width), BF16)] * 2
    scratch = [pltpu.VMEM((imgs, width), F32)]
    if first:
        outs += [jax.ShapeDtypeStruct((k, imgs), BF16)] * 2
        scratch = [pltpu.VMEM((k, imgs), F32), pltpu.VMEM((k, width), F32)] + scratch
        scratch += [pltpu.SemaphoreType.DMA((2, len(cuts)))]
    return pl.pallas_call(
        functools.partial(scores_kernel, g, m, cuts, first),
        out_shape=outs,
        in_specs=[HBM, HBM] if first else [VMEM] * 3,
        out_specs=[VMEM] * len(outs),
        scratch_shapes=scratch,
        cost_estimate=pl.CostEstimate(flops=6 * k * imgs * width, bytes_accessed=4 * k * width, transcendentals=0),
        compiler_params=pltpu.CompilerParams(vmem_limit_bytes=20 << 20),
        name="scores",
    )(*([feat, table] if first else [table, *halves]))


def table_kernel(g, m, cuts, chunk, *refs):
    f_hi, f_lo, mine, far = refs[:4]
    out, token, out_v, rhs, sems = refs[-5:]
    token[...] = jnp.zeros_like(token)
    imgs, width = rhs.shape[0] // 3, rhs.shape[1]
    n = g * m
    rows = imgs // n
    for p, block in enumerate(blocks(g, m, f"grads{chunk}")):
        src, q = (mine, p) if p < n // 2 else (far, p - n // 2)
        hi, lo = split(src[q * rows:(q + 1) * rows])
        for j, part in enumerate((hi, lo, hi)):
            rhs[pl.ds(pl.multiple_of(block * rows + j * imgs, rows), rows)] = part
    copies = []
    for i, (at, size) in enumerate(cuts):
        s = slice(at, at + size)
        a_hi = f_hi[s]
        out_v[s] = product(jnp.concatenate([a_hi, a_hi, f_lo[s]], axis=1), rhs[...], 1, 0)
        copy = pltpu.make_async_copy(
            out_v.at[pl.ds(at, size)],
            out.at[pl.ds(at, size), pl.ds(chunk * width, width)],
            sems.at[i],
        )
        copy.start()
        copies.append(copy)
    for copy in copies:
        copy.wait()


def table_call(g, m, f_hi, f_lo, piece, chunk, onto=None, depth=752):
    k, imgs = f_hi.shape
    width = piece[0].shape[1]
    cuts = cuts_of(k, depth)
    extra = [] if onto is None else [onto]
    return pl.pallas_call(
        functools.partial(table_kernel, g, m, cuts, chunk),
        out_shape=[jax.ShapeDtypeStruct((k, width * CHUNKS), F32), jax.ShapeDtypeStruct((8, 128), F32)],
        in_specs=[VMEM] * 4 + [HBM] * len(extra),
        out_specs=[HBM, VMEM],
        scratch_shapes=[
            pltpu.VMEM((k, width), F32),
            pltpu.VMEM((3 * imgs, width), BF16),
            pltpu.SemaphoreType.DMA((len(cuts),)),
        ],
        input_output_aliases={4: 0} if extra else {},
        cost_estimate=pl.CostEstimate(flops=6 * k * imgs * width, bytes_accessed=4 * k * width, transcendentals=0),
        compiler_params=pltpu.CompilerParams(vmem_limit_bytes=24 << 20),
        name="grad_table",
    )(f_hi, f_lo, *piece, *extra)


def features_kernel(g, m, parts, *refs):
    tables, pieces = refs[:2 * CHUNKS], refs[2 * CHUNKS:4 * CHUNKS]
    outs, (rows_v, rhs) = refs[4 * CHUNKS + 1:-2], refs[-2:]
    n = g * m
    imgs, width = rows_v.shape
    rows = imgs // n
    shift = 0 if parts == 1 else (1 - lax.axis_index("rot")) * (n // 2)
    for c in range(CHUNKS):
        mine, far = pieces[2 * c:2 * c + 2]
        for p, block in enumerate(blocks(g, m, f"grads{c}")):
            src, q = (mine, p) if p < n // 2 else (far, p - n // 2)
            place = lax.rem(block + shift, n)
            rows_v[pl.ds(pl.multiple_of(place * rows, rows), rows)] = src[q * rows:(q + 1) * rows]
        hi, lo = split(rows_v[...].T)
        for j, part in enumerate((hi, lo, hi)):
            rhs[(3 * c + j) * width:(3 * c + j + 1) * width] = part
    left = []
    for c in range(CHUNKS):
        hi, lo = tables[2 * c][...], tables[2 * c + 1][...]
        left += [hi, hi, lo]
    got = product(jnp.concatenate(left, axis=1), rhs[...], 1, 0)
    share = imgs // parts
    for i, out in enumerate(outs):
        out[...] = got[:, i * share:(i + 1) * share]


def features_call(g, m, tables, pieces, parts, after):
    k, width = tables[0].shape
    imgs = 2 * pieces[0].shape[0]
    return pl.pallas_call(
        functools.partial(features_kernel, g, m, parts),
        out_shape=[jax.ShapeDtypeStruct((k, imgs // parts), F32)] * parts,
        in_specs=[VMEM] * (len(tables) + len(pieces) + 1),
        out_specs=[VMEM] * parts,
        scratch_shapes=[pltpu.VMEM((imgs, width), F32), pltpu.VMEM((3 * CHUNKS * width, imgs), BF16)],
        cost_estimate=pl.CostEstimate(
            flops=6 * k * imgs * width * CHUNKS, bytes_accessed=4 * k * width * CHUNKS, transcendentals=0
        ),
        compiler_params=pltpu.CompilerParams(vmem_limit_bytes=24 << 20),
        name="grad_features",
    )(*tables, *pieces, after)


def join_kernel(g, mine, other, out):
    rows = mine.shape[0]
    cube = lax.div(lax.axis_index("coef"), g)
    out[pl.ds(pl.multiple_of(cube * rows, rows), rows)] = mine[...]
    out[pl.ds(pl.multiple_of((1 - cube) * rows, rows), rows)] = other[...]


def join_call(g, mine, other):
    rows, cols = mine.shape
    return pl.pallas_call(
        functools.partial(join_kernel, g),
        out_shape=jax.ShapeDtypeStruct((2 * rows, cols), mine.dtype),
        in_specs=[VMEM] * 2,
        out_specs=VMEM,
        compiler_params=pltpu.CompilerParams(vmem_limit_bytes=4 << 20),
        name="join",
    )(mine, other)


def solution(mesh):
    n = mesh.shape["coef"]
    r = mesh.shape["rot"]
    g = math.gcd(n, 8)
    m = n // g
    outer = [[a * g + b for a in range(m)] for b in range(g)]
    swap = [(i, (i + g) % n) for i in range(n)]
    rot_swap = [(0, 1), (1, 0)]
    steps = g.bit_length() - 1

    def exchange(x, use, step):
        perm = [(i * r + c, (i ^ masks_of(g, use, c % 2)[step]) * r + c) for i in range(n) for c in range(r)]
        return lax.ppermute(x, ("coef", "rot"), perm)

    def add_cubes(x):
        if m == 1:
            return x
        if m == 2:
            return x + lax.ppermute(x, "coef", swap)
        return lax.psum(x, "coef", axis_index_groups=outer)

    def join_cubes(x):
        if m == 1:
            return x
        if m == 2:
            return join_call(g, x, lax.ppermute(x, "coef", swap))
        return lax.all_gather(x, "coef", axis_index_groups=outer, tiled=True)

    def reduce(use, keep, send):
        x = keep + exchange(send, use, 0)
        for step in range(1, steps):
            half = x.shape[0] // 2
            x = x[:half] + exchange(x[half:], use, step)
        return add_cubes(x)

    def gather(use, x):
        for step in reversed(range(1, steps)):
            x = jnp.concatenate([x, exchange(x, use, step)])
        return x, exchange(x, use, 0)

    def on_device(features, table, targets):
        imgs, k = features.shape
        rots = table.shape[0]
        width = rots // CHUNKS
        scale = logit_gain / math.sqrt(k * n)
        features = pltpu.with_memory_space_constraint(features.T, pltpu.HBM)
        later = table.T
        table = pltpu.with_memory_space_constraint(table.T, pltpu.HBM)
        goal = join_cubes(targets)

        keep, send, *rest = scores_call(g, m, table, feat=features)
        tables, halves = rest[:2], rest[2:]
        last_keep, last_send, *more = scores_call(g, m, later, halves=halves)
        tables = tables + more
        scores = [scale * reduce("scores0", keep, send), scale * reduce("scores1", last_keep, last_send)]

        top = functools.reduce(jnp.maximum, [jnp.max(s, axis=1, keepdims=True) for s in scores])
        expo = [jnp.exp(s - top) for s in scores]
        total = sum(jnp.sum(e, axis=1, keepdims=True) for e in expo)
        if r == 2:
            both = jnp.concatenate([top, total], axis=1)
            far = lax.ppermute(both, "rot", rot_swap)
            far_top, far_total = far[:, :1], far[:, 1:]
            row_max = jnp.maximum(top, far_top)
            ours = jnp.exp(top - row_max)
            row_sum = total * ours + far_total * jnp.exp(far_top - row_max)
        else:
            row_max = lax.pmax(top, "rot")
            ours = jnp.exp(top - row_max)
            row_sum = lax.psum(total * ours, "rot")
        norm = ours / row_sum
        pieces = []
        for c, e in enumerate(expo):
            grad = (scale * loss_scale) * (e * norm - goal[:, c * width:(c + 1) * width])
            pieces.append(gather(f"grads{c}", grad))

        grad_table, done = table_call(g, m, *halves, pieces[0], 0)
        flat = [x for piece in pieces for x in piece]
        if r == 2:
            send, keep = features_call(g, m, tables, flat, 2, done)
            grad_features = keep + lax.ppermute(send, "rot", rot_swap)
        else:
            (whole,) = features_call(g, m, tables, flat, 1, done)
            grad_features = lax.psum_scatter(whole, "rot", scatter_dimension=1, tiled=True)
        grad_table, _ = table_call(g, m, *halves, pieces[1], 1, grad_table)
        return (grad_features.T, grad_table.T)

    return jax.shard_map(
        on_device,
        mesh=mesh,
        in_specs=(P(None, "coef"), P("rot", "coef"), P("coef", "rot")),
        out_specs=(P("rot", "coef"), P("rot", "coef")),
        check_vma=False,
    )
```

```python
import functools
import math

import jax
import jax.numpy as jnp
from jax import lax
from jax.experimental import pallas as pl
from jax.experimental.pallas import tpu as pltpu
from jax.sharding import PartitionSpec as P

logit_gain = 4.0
loss_scale = 64.0

F32, BF16 = jnp.float32, jnp.bfloat16
HBM = pl.BlockSpec(memory_space=pltpu.HBM)
VMEM = pl.BlockSpec(memory_space=pltpu.VMEM)
CHUNKS = 2


def split(x):
    hi = x.astype(BF16)
    return hi, (x - hi.astype(F32)).astype(BF16)


def product(a, b, da, db):
    return lax.dot_general(a, b, (((da,), (db,)), ((), ())), preferred_element_type=F32)


def cuts_of(k, most):
    return [(a, min(most, k - a)) for a in range(0, k, most)]


ORDERS = {
    "scores0": ((0, 2, 1), (1, 2, 0)),
    "scores1": ((0, 2, 1), (1, 2, 0)),
    "grads0": ((0, 1, 2), (1, 2, 0)),
    "grads1": ((0, 1, 2), (1, 2, 0)),
}


def masks_of(g, use, odd):
    return [1 << b for b in ORDERS[use][odd] if 1 << b < g]


def blocks(g, m, use):
    me, core = lax.axis_index("coef"), lax.axis_index("rot")
    odd = lax.rem(core, 2)
    inner = lax.rem(me, g)
    found = []
    for q in range(g):
        far = []
        for order in (0, 1):
            steps = masks_of(g, use, order)
            far.append(sum(bit for s, bit in enumerate(reversed(steps)) if q >> s & 1))
        flip = jnp.where(odd == 1, far[1], far[0])
        for a in range(m):
            found.append(a * g + jnp.bitwise_xor(inner, flip))
    return found


def scores_kernel(g, m, cuts, first, *refs):
    if first:
        feat, table, keep, send, t_hi, t_lo, f_hi, f_lo, feat_v, table_v, acc, sems = refs
    else:
        table_v, f_hi, f_lo, keep, send, t_hi, t_lo, acc = refs
    width = keep.shape[1]
    copies = [[] for _ in cuts]
    if first:
        for i, (at, size) in enumerate(cuts):
            s = pl.ds(at, size)
            copies[i] = [
                pltpu.make_async_copy(table.at[s, pl.ds(0, width)], table_v.at[s], sems.at[0, i]),
                pltpu.make_async_copy(feat.at[s], feat_v.at[s], sems.at[1, i]),
            ]
            for c in copies[i]:
                c.start()
    for i, (at, size) in enumerate(cuts):
        for c in copies[i]:
            c.wait()
        s = slice(at, at + size)
        if first:
            a_hi, a_lo = split(feat_v[s])
            f_hi[s], f_lo[s] = a_hi, a_lo
        else:
            a_hi, a_lo = f_hi[s], f_lo[s]
        b_hi, b_lo = split(table_v[s] if first else table_v[s, width:2 * width])
        t_hi[s], t_lo[s] = b_hi, b_lo
        left = jnp.concatenate([a_hi, a_hi, a_lo], axis=0)
        right = jnp.concatenate([b_hi, b_lo, b_hi], axis=0)
        got = product(left, right, 0, 0)
        if i == 0:
            acc[...] = got
        else:
            acc[...] += got
    rows = acc.shape[0] // (g * m)
    half = g * m // 2
    for p, block in enumerate(blocks(g, m, "scores0" if first else "scores1")):
        out, q = (keep, p) if p < half else (send, p - half)
        out[q * rows:(q + 1) * rows] = acc[pl.ds(pl.multiple_of(block * rows, rows), rows)]


def scores_call(g, m, table, feat=None, halves=None, depth=512):
    first = halves is None
    k, width = table.shape
    width //= CHUNKS
    imgs = (feat if first else halves[0]).shape[1]
    cuts = cuts_of(k, depth)
    outs = [jax.ShapeDtypeStruct((imgs // 2, width), F32)] * 2 + [jax.ShapeDtypeStruct((k, width), BF16)] * 2
    scratch = [pltpu.VMEM((imgs, width), F32)]
    if first:
        outs += [jax.ShapeDtypeStruct((k, imgs), BF16)] * 2
        scratch = [pltpu.VMEM((k, imgs), F32), pltpu.VMEM((k, width), F32)] + scratch
        scratch += [pltpu.SemaphoreType.DMA((2, len(cuts)))]
    return pl.pallas_call(
        functools.partial(scores_kernel, g, m, cuts, first),
        out_shape=outs,
        in_specs=[HBM, HBM] if first else [VMEM] * 3,
        out_specs=[VMEM] * len(outs),
        scratch_shapes=scratch,
        cost_estimate=pl.CostEstimate(flops=6 * k * imgs * width, bytes_accessed=4 * k * width, transcendentals=0),
        compiler_params=pltpu.CompilerParams(vmem_limit_bytes=20 << 20),
        name="scores",
    )(*([feat, table] if first else [table, *halves]))


def table_kernel(g, m, cuts, chunk, *refs):
    f_hi, f_lo, mine, far = refs[:4]
    out, token, out_v, rhs, sems = refs[-5:]
    token[...] = jnp.zeros_like(token)
    imgs, width = rhs.shape[0] // 3, rhs.shape[1]
    n = g * m
    rows = imgs // n
    for p, block in enumerate(blocks(g, m, f"grads{chunk}")):
        src, q = (mine, p) if p < n // 2 else (far, p - n // 2)
        hi, lo = split(src[q * rows:(q + 1) * rows])
        for j, part in enumerate((hi, lo, hi)):
            rhs[pl.ds(pl.multiple_of(block * rows + j * imgs, rows), rows)] = part
    copies = []
    for i, (at, size) in enumerate(cuts):
        s = slice(at, at + size)
        a_hi = f_hi[s]
        out_v[s] = product(jnp.concatenate([a_hi, a_hi, f_lo[s]], axis=1), rhs[...], 1, 0)
        copy = pltpu.make_async_copy(
            out_v.at[pl.ds(at, size)],
            out.at[pl.ds(at, size), pl.ds(chunk * width, width)],
            sems.at[i],
        )
        copy.start()
        copies.append(copy)
    for copy in copies:
        copy.wait()


def table_call(g, m, f_hi, f_lo, piece, chunk, onto=None, depth=752):
    k, imgs = f_hi.shape
    width = piece[0].shape[1]
    cuts = cuts_of(k, depth)
    extra = [] if onto is None else [onto]
    return pl.pallas_call(
        functools.partial(table_kernel, g, m, cuts, chunk),
        out_shape=[jax.ShapeDtypeStruct((k, width * CHUNKS), F32), jax.ShapeDtypeStruct((8, 128), F32)],
        in_specs=[VMEM] * 4 + [HBM] * len(extra),
        out_specs=[HBM, VMEM],
        scratch_shapes=[
            pltpu.VMEM((k, width), F32),
            pltpu.VMEM((3 * imgs, width), BF16),
            pltpu.SemaphoreType.DMA((len(cuts),)),
        ],
        input_output_aliases={4: 0} if extra else {},
        cost_estimate=pl.CostEstimate(flops=6 * k * imgs * width, bytes_accessed=4 * k * width, transcendentals=0),
        compiler_params=pltpu.CompilerParams(vmem_limit_bytes=24 << 20),
        name="grad_table",
    )(f_hi, f_lo, *piece, *extra)


def features_kernel(g, m, parts, *refs):
    tables, pieces = refs[:2 * CHUNKS], refs[2 * CHUNKS:4 * CHUNKS]
    outs, (rows_v, rhs) = refs[4 * CHUNKS + 1:-2], refs[-2:]
    n = g * m
    imgs, width = rows_v.shape
    rows = imgs // n
    shift = 0 if parts == 1 else (1 - lax.axis_index("rot")) * (n // 2)
    for c in range(CHUNKS):
        mine, far = pieces[2 * c:2 * c + 2]
        for p, block in enumerate(blocks(g, m, f"grads{c}")):
            src, q = (mine, p) if p < n // 2 else (far, p - n // 2)
            place = lax.rem(block + shift, n)
            rows_v[pl.ds(pl.multiple_of(place * rows, rows), rows)] = src[q * rows:(q + 1) * rows]
        hi, lo = split(rows_v[...].T)
        for j, part in enumerate((hi, lo, hi)):
            rhs[(3 * c + j) * width:(3 * c + j + 1) * width] = part
    left = []
    for c in range(CHUNKS):
        hi, lo = tables[2 * c][...], tables[2 * c + 1][...]
        left += [hi, hi, lo]
    got = product(jnp.concatenate(left, axis=1), rhs[...], 1, 0)
    share = imgs // parts
    for i, out in enumerate(outs):
        out[...] = got[:, i * share:(i + 1) * share]


def features_call(g, m, tables, pieces, parts, after):
    k, width = tables[0].shape
    imgs = 2 * pieces[0].shape[0]
    return pl.pallas_call(
        functools.partial(features_kernel, g, m, parts),
        out_shape=[jax.ShapeDtypeStruct((k, imgs // parts), F32)] * parts,
        in_specs=[VMEM] * (len(tables) + len(pieces) + 1),
        out_specs=[VMEM] * parts,
        scratch_shapes=[pltpu.VMEM((imgs, width), F32), pltpu.VMEM((3 * CHUNKS * width, imgs), BF16)],
        cost_estimate=pl.CostEstimate(
            flops=6 * k * imgs * width * CHUNKS, bytes_accessed=4 * k * width * CHUNKS, transcendentals=0
        ),
        compiler_params=pltpu.CompilerParams(vmem_limit_bytes=24 << 20),
        name="grad_features",
    )(*tables, *pieces, after)


def join_kernel(g, mine, other, out):
    rows = mine.shape[0]
    cube = lax.div(lax.axis_index("coef"), g)
    out[pl.ds(pl.multiple_of(cube * rows, rows), rows)] = mine[...]
    out[pl.ds(pl.multiple_of((1 - cube) * rows, rows), rows)] = other[...]


def join_call(g, mine, other):
    rows, cols = mine.shape
    return pl.pallas_call(
        functools.partial(join_kernel, g),
        out_shape=jax.ShapeDtypeStruct((2 * rows, cols), mine.dtype),
        in_specs=[VMEM] * 2,
        out_specs=VMEM,
        compiler_params=pltpu.CompilerParams(vmem_limit_bytes=4 << 20),
        name="join",
    )(mine, other)


def solution(mesh):
    n = mesh.shape["coef"]
    r = mesh.shape["rot"]
    g = math.gcd(n, 8)
    m = n // g
    outer = [[a * g + b for a in range(m)] for b in range(g)]
    swap = [(i, (i + g) % n) for i in range(n)]
    rot_swap = [(0, 1), (1, 0)]
    steps = g.bit_length() - 1

    def exchange(x, use, step):
        perm = [(i * r + c, (i ^ masks_of(g, use, c % 2)[step]) * r + c) for i in range(n) for c in range(r)]
        return lax.ppermute(x, ("coef", "rot"), perm)

    def add_cubes(x):
        if m == 1:
            return x
        if m == 2:
            return x + lax.ppermute(x, "coef", swap)
        return lax.psum(x, "coef", axis_index_groups=outer)

    def join_cubes(x):
        if m == 1:
            return x
        if m == 2:
            return join_call(g, x, lax.ppermute(x, "coef", swap))
        return lax.all_gather(x, "coef", axis_index_groups=outer, tiled=True)

    def reduce(use, keep, send):
        x = keep + exchange(send, use, 0)
        for step in range(1, steps):
            half = x.shape[0] // 2
            x = x[:half] + exchange(x[half:], use, step)
        return add_cubes(x)

    def gather(use, x):
        for step in reversed(range(1, steps)):
            x = jnp.concatenate([x, exchange(x, use, step)])
        return x, exchange(x, use, 0)

    def on_device(features, table, targets):
        imgs, k = features.shape
        rots = table.shape[0]
        width = rots // CHUNKS
        scale = logit_gain / math.sqrt(k * n)
        features = pltpu.with_memory_space_constraint(features.T, pltpu.HBM)
        later = table.T
        table = pltpu.with_memory_space_constraint(table.T, pltpu.HBM)
        goal = join_cubes(targets)

        keep, send, *rest = scores_call(g, m, table, feat=features)
        tables, halves = rest[:2], rest[2:]
        last_keep, last_send, *more = scores_call(g, m, later, halves=halves)
        tables = tables + more
        scores = [scale * reduce("scores0", keep, send), scale * reduce("scores1", last_keep, last_send)]

        top = functools.reduce(jnp.maximum, [jnp.max(s, axis=1, keepdims=True) for s in scores])
        expo = [jnp.exp(s - top) for s in scores]
        total = sum(jnp.sum(e, axis=1, keepdims=True) for e in expo)
        if r == 2:
            both = jnp.concatenate([top, total], axis=1)
            far = lax.ppermute(both, "rot", rot_swap)
            far_top, far_total = far[:, :1], far[:, 1:]
            row_max = jnp.maximum(top, far_top)
            ours = jnp.exp(top - row_max)
            row_sum = total * ours + far_total * jnp.exp(far_top - row_max)
        else:
            row_max = lax.pmax(top, "rot")
            ours = jnp.exp(top - row_max)
            row_sum = lax.psum(total * ours, "rot")
        norm = ours / row_sum
        pieces = []
        for c, e in enumerate(expo):
            grad = (scale * loss_scale) * (e * norm - goal[:, c * width:(c + 1) * width])
            pieces.append(gather(f"grads{c}", grad))

        grad_table, done = table_call(g, m, *halves, pieces[0], 0)
        flat = [x for piece in pieces for x in piece]
        if r == 2:
            send, keep = features_call(g, m, tables, flat, 2, done)
            grad_features = keep + lax.ppermute(send, "rot", rot_swap)
        else:
            (whole,) = features_call(g, m, tables, flat, 1, done)
            grad_features = lax.psum_scatter(whole, "rot", scatter_dimension=1, tiled=True)
        grad_table, _ = table_call(g, m, *halves, pieces[1], 1, grad_table)
        return (grad_features.T, grad_table.T)

    return jax.shard_map(
        on_device,
        mesh=mesh,
        in_specs=(P(None, "coef"), P("rot", "coef"), P("coef", "rot")),
        out_specs=(P("rot", "coef"), P("rot", "coef")),
        check_vma=False,
    )
```
